128 devices in a mesh: inner: 8 (over x_hi, y), outer: 16 (over x_lo, z, core).
Axes of the slice: x: 4 (x_hi: 2, x_lo: 2; x = x_hi * 2 + x_lo), y: 4, z: 4, core: 2. Of those that a mesh axis runs over, the one named last changes fastest.
Arguments:
- queries: bfloat16 [16, 4096, 768], P('outer', 'inner'), may hold values from -8 to 8
- key_rows: bfloat16 [16, 4096, 768], P('outer', 'inner'), may hold values from -8 to 8
- values: bfloat16 [16, 4096, 768], P('outer', 'inner'), may hold values from -6 to 6
- out_weight: bfloat16 [768, 768], replicated, may hold values from -0.21875 to 0.21875
Outputs:
- attention_out: bfloat16 [16, 4096, 768], P('outer', 'inner')
The draws below stay inside these ranges and needn't reach their ends.
All inputs are finite; a program needn't handle non-finite values.
Results may differ from the reference program's by a relative error of at most 0.0052.
Values may be sent and summed in bfloat16 or wider, within the bound.
A program may use at most 64 MiB of HBM per device.

```python
import jax
import jax.numpy as jnp
from jax import lax

HEADS = 12
HEAD_DIM = 64
D = 768
TOK_DEV = 512
GSTEP = 64
IBITS = 3
SEG_ROWS = 4096
N_INNER = 8
N_OUTER = 16


def base_rows(key):
    shape_rows = (N_OUTER, N_INNER, TOK_DEV, D)
    rows = 2.0 * jnp.clip(jax.random.normal(key, shape_rows, jnp.float32), -4.0, 4.0)
    return rows


def draw_key_rows(key, part):
    rows = base_rows(jax.random.fold_in(key, 31))
    return rows.reshape(N_OUTER, N_INNER * TOK_DEV, D).astype(jnp.bfloat16)


def draw_queries(key, part):
    rows = base_rows(jax.random.fold_in(key, 41))
    return rows.reshape(N_OUTER, N_INNER * TOK_DEV, D).astype(jnp.bfloat16)


def shard_levels(rng, extent, cuts, least, top_value):
    level, own = 1.0, jax.random.fold_in(rng, 6)
    for axis_at, blocks in cuts:
        heights = jnp.exp(jax.random.uniform(jax.random.fold_in(own, axis_at), (blocks,), jnp.float32, least / len(cuts), top_value / len(cuts)))
        level = level * jnp.repeat(heights, extent[axis_at] // blocks).reshape([-1 if axis == axis_at else 1 for axis in range(len(extent))])
    return level


def normal_values(own_key, shape, deviation, reach, pieces=(), kind=jnp.bfloat16):
    factor_of = shard_levels(own_key, shape, pieces, -0.22, 0.18) if pieces else 1.0
    values = jax.random.normal(own_key, shape, jnp.float32) * deviation * factor_of
    return jnp.minimum(jnp.maximum(values, -reach), reach).astype(kind)


def setup_inputs(seed: int = 0) -> dict:
    seeds = jax.random.split(jax.random.key(seed), 5)
    return {
        "queries": draw_queries(jax.random.fold_in(seeds[4], 71), 0),
        "key_rows": draw_key_rows(jax.random.fold_in(seeds[4], 71), 0),
        "values": normal_values(seeds[2], (N_OUTER, SEG_ROWS, D), 1.0, 6.0, ((0, 16), (1, 8))),
        "out_weight": normal_values(seeds[3], (D, D), D ** -0.5, 0.21875),
    }


def level_terms(query_rows, key_set, value_set):
    scale_factor = HEAD_DIM ** -0.5
    head_query = query_rows.astype(jnp.float32).reshape(TOK_DEV, HEADS, HEAD_DIM)
    head_keys = key_set.astype(jnp.float32).reshape(-1, HEADS, HEAD_DIM)
    head_values = value_set.astype(jnp.float32).reshape(-1, HEADS, HEAD_DIM)
    scores = jnp.einsum("thd,nhd->htn", head_query, head_keys) * scale_factor
    row_peak = jnp.max(scores, axis=2, keepdims=True)
    expo_rows = jnp.exp(scores - row_peak)
    row_total = jnp.sum(expo_rows, axis=2, keepdims=True)
    weights = lax.optimization_barrier(expo_rows.astype(jnp.bfloat16)).astype(jnp.float32)
    numerator = jnp.einsum("htn,nhd->htd", weights, head_values)
    return row_peak, row_total, numerator


def merge_levels(all_terms):
    overall_peak = jnp.max(jnp.stack([entry[0] for entry in all_terms]), axis=0)
    numer_sum = jnp.zeros_like(all_terms[0][2])
    denom_sum = jnp.zeros_like(all_terms[0][1])
    for entry in all_terms:
        factor = jnp.exp(entry[0] - overall_peak)
        numer_sum = numer_sum + factor * entry[2]
        denom_sum = denom_sum + factor * entry[1]
    return numer_sum / denom_sum


def reference(queries, key_rows, values, out_weight):
    flat_queries = queries.reshape(-1, D)
    flat_keys = key_rows.reshape(-1, D)
    flat_values = values.reshape(-1, D)
    global_keys = flat_keys[::GSTEP]
    global_values = flat_values[::GSTEP]
    device_count = N_INNER * N_OUTER

    def per_device(device):
        device = device.astype(jnp.int32)
        query_rows = lax.dynamic_slice_in_dim(flat_queries, (device * TOK_DEV).astype(jnp.int32), TOK_DEV, 0)
        collected = []
        for level_index in range(IBITS + 2):
            stride = 2 ** level_index
            span_rows = stride * TOK_DEV
            row_start = ((device // stride) * span_rows).astype(jnp.int32)
            seg_keys = lax.dynamic_slice_in_dim(flat_keys, row_start, span_rows, 0)[::stride]
            seg_values = lax.dynamic_slice_in_dim(flat_values, row_start, span_rows, 0)[::stride]
            collected.append(level_terms(query_rows, seg_keys, seg_values))
        collected.append(level_terms(query_rows, global_keys, global_values))
        merged = merge_levels(collected)
        attended = merged.transpose(1, 0, 2).reshape(TOK_DEV, D).astype(jnp.bfloat16)
        return jnp.dot(attended, out_weight, preferred_element_type=jnp.float32).astype(jnp.bfloat16)

    result = lax.map(per_device, jnp.arange(device_count, dtype=jnp.int32))
    return result.reshape(N_OUTER, N_INNER * TOK_DEV, D)
```

```python
import jax
import jax.numpy as jnp
import numpy as np
from jax import lax
from jax.experimental import pallas as pl
from jax.experimental.pallas import tpu as pltpu
from jax.sharding import PartitionSpec as P

HEADS = 12
HEAD_DIM = 64
D = 768
T = 512
MESH = pl.DeviceIdType.MESH
BLK = 256
GROW = 1536

A0, B30, C0, D0, D1 = 512, 576, 640, 704, 736
B20, C1, A1, D2, D3 = 768, 832, 896, 960, 992
A2, B31, C2, D4, D5 = 1024, 1088, 1152, 1216, 1248
A3, B21, C3, D6, D7 = 1280, 1344, 1408, 1472, 1504


def key_weights():
    w = np.ones((10, BLK), np.float32)
    flat = w.reshape(-1)
    tok = np.arange(T)
    for level in range(1, 5):
        flat[:T] += tok % (1 << level) == 0
    for base, top in ((A0, 4), (B30, 3), (B20, 3), (C0, 2), (C1, 2), (C2, 2), (C3, 2)):
        flat[base : base + 32] = top
        flat[base + 32 : base + 64] = top - 1
    flat[A1 : A1 + 64] = 2
    return w


class Links:
    def __init__(self, send_sem, recv_sem):
        self.send_sem, self.recv_sem, self.count, self.sent = send_sem, recv_sem, 0, []

    def make(self, src, dst, device):
        i = self.count
        self.count += 1
        return pltpu.make_async_remote_copy(
            src_ref=src,
            dst_ref=dst,
            send_sem=self.send_sem.at[i],
            recv_sem=self.recv_sem.at[i],
            device_id=device,
            device_id_type=MESH,
        )


def kernel(
    q_hbm, k_hbm, v_hbm, wout_hbm, wt_ref, o_ref,
    ch, snd, qv, qm, acc, ms, blk, rb, wout, att, send_sem, recv_sem, loc_sem,
):
    inner, outer = lax.axis_index("inner"), lax.axis_index("outer")
    y, xh = lax.rem(inner, 4), lax.div(inner, 4)
    core = lax.rem(outer, 2)
    z = lax.rem(lax.div(outer, 2), 4)
    xl = lax.div(outer, 8)
    x = xh * 2 + xl

    def dev(x, y, z, core):
        return (lax.div(x, 2) * 4 + y, lax.rem(x, 2) * 8 + z * 2 + core)

    xs = [lax.rem(x + i, 4) for i in range(4)]
    ys = [y, lax.rem(y, 2) * -2 + 1 + y, lax.rem(y + 2, 4), 3 - y]
    zs = [lax.rem(z + i, 4) for i in range(4)]
    to_core = dev(x, y, z, 1 - core)
    to_x = [None] + [dev(xs[i], y, z, core) for i in (1, 2, 3)]
    to_y = [None] + [dev(x, ys[i], z, core) for i in (1, 2, 3)]
    to_up, to_down = dev(x, y, zs[1], core), dev(x, y, zs[3], core)
    partners = [to_core] + to_x[1:] + to_y[1:] + [to_up, to_down]

    loads = [
        pltpu.make_async_copy(k_hbm, ch.at[0, pl.ds(0, T)], loc_sem.at[0]),
        pltpu.make_async_copy(v_hbm, ch.at[1, pl.ds(0, T)], loc_sem.at[1]),
        pltpu.make_async_copy(q_hbm, qv, loc_sem.at[2]),
        pltpu.make_async_copy(wout_hbm, wout, loc_sem.at[3]),
    ]
    for load in loads:
        load.start()
    barrier = pltpu.get_barrier_semaphore()
    for device in partners:
        pl.semaphore_signal(barrier, inc=1, device_id=device, device_id_type=MESH)

    row = lax.broadcasted_iota(jnp.int32, (BLK, T), 0)
    col = lax.broadcasted_iota(jnp.int32, (BLK, T), 1)
    token = jnp.where(
        row < 32,
        row * 16,
        jnp.where(row < 64, row * 16 - 504, jnp.where(row < 128, row * 8 - 508, row * 4 - 510)),
    )
    pick = jnp.where(col == token, 1.0, 0.0).astype(jnp.bfloat16)
    grow = lax.broadcasted_iota(jnp.int32, (16, T), 0)
    gcol = lax.broadcasted_iota(jnp.int32, (16, T), 1)
    gpick = jnp.where(gcol == (grow - core * 8) * 64, 1.0, 0.0)
    gpick = jnp.where((grow < 8) == (core == 0), gpick, 0.0).astype(jnp.bfloat16)
    for i in range(2):
        loads[i].wait()
        own = ch[i, 0:T, :]
        snd[i] = jnp.dot(pick, own, preferred_element_type=jnp.float32).astype(jnp.bfloat16)
        blk[i] = jnp.dot(gpick, own, preferred_element_type=jnp.float32).astype(jnp.bfloat16)

    links = Links(send_sem, recv_sem)

    def piece(src_row, dst_row, rows, device, from_snd=False):
        src = (snd if from_snd else ch).at[:, pl.ds(src_row, rows)]
        return links.make(src, ch.at[:, pl.ds(dst_row, rows)], device)

    def gpiece(start, rows, device, land=None, part=None):
        part = core if part is None else part
        where = pl.ds(pl.multiple_of(start, 16), rows)
        return links.make(ch.at[part, where], ch.at[part, where], device)

    plane = [GROW + zz * BLK for zz in zs]
    slot = plane[0] + y * 64 + x * 16
    c_a0 = piece(0, A0, 64, to_y[1], True)
    c_b30 = piece(0, B30, 64, to_y[3], True)
    c_c0 = piece(0, C0, 64, to_x[2], True)
    c_d0 = piece(0, D0, 32, to_core, True)
    c_a1 = piece(64, A1, 64, to_y[1], True)
    c_b31 = piece(64, B31, 64, to_y[3], True)
    c_a2 = piece(128, A2, 64, to_y[1], True)
    c_a3 = piece(192, A3, 64, to_y[1], True)
    c_b20 = piece(A0, B20, 64, to_y[3])
    c_c1 = piece(A0, C1, 64, to_x[2])
    c_c2 = piece(B30, C2, 64, to_x[2])
    c_c3 = piece(B20, C3, 64, to_x[2])
    c_b21 = piece(A1, B21, 64, to_y[3])
    c_d1 = piece(A0, D1, 32, to_core)
    c_d2 = piece(B30, D2, 32, to_core)
    c_d3 = piece(B20, D3, 32, to_core)
    c_d4 = piece(C0, D4, 32, to_core)
    c_d5 = piece(C1, D5, 32, to_core)
    c_d6 = piece(C2, D6, 32, to_core)
    c_d7 = piece(C3, D7, 32, to_core)
    e0 = links.make(blk.at[1 - core], rb, to_core)
    e1 = [gpiece(slot, 16, to_x[i]) for i in (1, 2, 3)]
    e2 = [gpiece(plane[0] + y * 64, 64, to_y[i]) for i in (1, 2, 3)]
    e3 = [gpiece(plane[0], BLK, to_up), gpiece(plane[0], BLK, to_down)]
    e4 = [gpiece(plane[3], 128, to_up), gpiece(plane[1] + 128, 128, to_down)]
    f0 = gpiece(plane[0], BLK, to_core)
    f1 = gpiece(plane[1], BLK, to_core)
    f3 = gpiece(plane[3], BLK, to_core)
    f2 = gpiece(plane[2], BLK, to_core)
    everything = [
        c_a0, c_b30, c_c0, c_d0, c_a1, c_b31, c_a2, c_a3, c_b20, c_c1, c_c2, c_c3, c_b21,
        c_d1, c_d2, c_d3, c_d4, c_d5, c_d6, c_d7, e0, *e1, *e2, *e3, *e4, f0, f1, f3, f2,
    ]

    def start(*copies):
        for copy in copies:
            copy.start()

    def arrived(*copies):
        for copy in copies:
            copy.wait_recv()

    pl.semaphore_wait(barrier, len(partners))
    start(e0, c_a0, c_b30, c_d0)

    lane = lax.broadcasted_iota(jnp.int32, (1, 128), 1)
    loads[2].wait()
    for p in range(HEADS // 2):
        q = qv[:, p * 128 : (p + 1) * 128] * jnp.bfloat16(HEAD_DIM**-0.5)
        zero = jnp.zeros_like(q)
        qm[2 * p] = jnp.where(lane < 64, q, zero)
        qm[2 * p + 1] = jnp.where(lane < 64, zero, q)
    acc[...] = jnp.zeros_like(acc)
    ms[...] = jnp.full_like(ms, -1e30)
    arrived(e0)
    ch[core, pl.ds(pl.multiple_of(slot, 16), 16), :] = blk[core] + rb[...]
    start(*e1, c_c0)

    def attend(r0):
        rows = pl.ds(pl.multiple_of(r0, BLK), BLK)
        weight = wt_ref[pl.ds(lax.div(r0, BLK), 1), :]
        for p in range(HEADS // 2):
            keys = ch[0, rows, p * 128 : (p + 1) * 128]
            vals = ch[1, rows, p * 128 : (p + 1) * 128]
            one = jnp.ones_like(vals)
            for h in range(2):
                n = 2 * p + h
                vx = jnp.where(lane < 64, vals, one) if h == 0 else jnp.where(lane < 64, one, vals)
                s = lax.dot_general(
                    qm[n], keys, (((1,), (1,)), ((), ())), preferred_element_type=jnp.float32
                )
                old = ms[n]
                new = jnp.maximum(old, jnp.max(s, axis=1, keepdims=True))
                e = jnp.exp(s - jnp.concatenate([new, new], axis=1)) * weight
                acc[n] = acc[n] * jnp.exp(old - new) + jnp.dot(
                    e.astype(jnp.bfloat16), vx, preferred_element_type=jnp.float32
                )
                ms[n] = new

    order = [0, BLK, A0, plane[0], B20, A2, plane[1], plane[3], A3, plane[2]]

    def step(j, carry):
        @pl.when(j == 1)
        def _():
            arrived(*e1)
            start(*e2, c_a1)

        @pl.when(j == 2)
        def _():
            arrived(c_a0)
            start(c_b20, c_c1, c_d1)
            arrived(c_b30)
            start(c_c2, c_d2, c_b31, c_a2, c_a3)
            arrived(c_c0)
            start(c_d4)
            arrived(c_d0, c_d1)

        @pl.when(j == 3)
        def _():
            arrived(*e2)
            start(*e3, f0)
            arrived(f0)

        @pl.when(j == 4)
        def _():
            arrived(c_b20)
            start(c_c3, c_d3)
            arrived(c_a1)
            start(c_b21)
            arrived(c_c1)
            start(c_d5)
            arrived(c_d2, c_d3)

        @pl.when(j == 5)
        def _():
            arrived(c_a2, c_b31, c_c2)
            start(c_d6)
            arrived(c_d4, c_d5)

        @pl.when(j == 6)
        def _():
            arrived(*e3)
            start(*e4, f1, f3)
            arrived(f1)

        @pl.when(j == 7)
        def _():
            arrived(f3)

        @pl.when(j == 8)
        def _():
            arrived(c_a3, c_b21, c_c3)
            start(c_d7)
            arrived(*e4)
            start(f2)
            arrived(c_d6, c_d7)

        @pl.when(j == 9)
        def _():
            arrived(f2)

        r0 = sum(jnp.where(j == i, at, 0) for i, at in enumerate(order))
        attend(r0)
        return carry

    lax.fori_loop(0, len(order), step, 0)

    for p in range(HEADS // 2):
        lo, hi = acc[2 * p], acc[2 * p + 1]
        both = jnp.where(lane < 64, lo / pltpu.roll(lo, 64, 1), hi / pltpu.roll(hi, 64, 1))
        att[:, p * 128 : (p + 1) * 128] = both.astype(jnp.bfloat16)
    loads[3].wait()
    o_ref[...] = jnp.dot(att[...], wout[...], preferred_element_type=jnp.float32).astype(jnp.bfloat16)
    for copy in everything:
        copy.wait_send()


N_COPIES = 35


def local(queries, key_rows, values, out_weight):
    anywhere = pl.BlockSpec(memory_space=pl.ANY)
    vmem = pl.BlockSpec(memory_space=pltpu.VMEM)
    bf16, f32 = jnp.bfloat16, jnp.float32
    out = pl.pallas_call(
        kernel,
        out_shape=jax.ShapeDtypeStruct((T, D), bf16),
        in_specs=[anywhere] * 4 + [vmem],
        out_specs=vmem,
        scratch_shapes=[
            pltpu.VMEM((2, 2560, D), bf16),
            pltpu.VMEM((2, BLK, D), bf16),
            pltpu.VMEM((T, D), bf16),
            pltpu.VMEM((HEADS, T, 128), bf16),
            pltpu.VMEM((HEADS, T, 128), f32),
            pltpu.VMEM((HEADS, T, 128), f32),
            pltpu.VMEM((2, 16, D), bf16),
            pltpu.VMEM((16, D), bf16),
            pltpu.VMEM((D, D), bf16),
            pltpu.VMEM((T, D), bf16),
            pltpu.SemaphoreType.DMA((N_COPIES,)),
            pltpu.SemaphoreType.DMA((N_COPIES,)),
            pltpu.SemaphoreType.DMA((4,)),
        ],
        compiler_params=pltpu.CompilerParams(
            collective_id=0, has_side_effects=True, vmem_limit_bytes=60 << 20
        ),
    )(queries[0], key_rows[0], values[0], out_weight, jnp.asarray(key_weights()))
    return out[None]


def solution(mesh):
    placed = P("outer", "inner", None)
    return jax.shard_map(
        local, mesh=mesh, in_specs=(placed, placed, placed, P()), out_specs=placed, check_vma=False
    )
```

```python
import jax
import jax.numpy as jnp
from jax import lax
from jax.experimental import pallas as pl
from jax.experimental.pallas import tpu as pltpu
from jax.sharding import PartitionSpec as P

HEADS = 12
HEAD_DIM = 64
D = 768
T = 512
MESH = pl.DeviceIdType.MESH
BLK = 256

ROW = {
    "B30": 512,
    "C0": 576,
    "A0": 640,
    "D1": 704,
    "D0": 736,
    "C3": 768,
    "B21": 832,
    "A2": 896,
    "D7": 960,
    "D2": 992,
    "C2": 1024,
    "A1": 1088,
    "B20": 1152,
    "D3": 1216,
    "D6": 1248,
    "A3": 1280,
    "C1": 1344,
    "B31": 1408,
    "D4": 1472,
    "D5": 1504,
}
GA, GBC, GD = 1536, 1792, 2304
FIRST = ("+e0",)
SECOND = ("+D0", "+A0", "+B30")
STEPS = (
    (256, "-e0", "+e12", "+e11", "+e13", "+C0"),
    (0, "-D0"),
    (512, "-e11", "-e13", "-e12", "+up0", "+e21", "+dn0", "+e23", "+e22", "+A1", "+A3", "+A2", "-A0", "+D1", "+B20", "+B31", "-B30", "+D2", "+C2", "+C1", "-D1", "-D2", "-C0", "+D4", "-e21", "+up1", "+dn1", "-up0", "-dn0", "-e23", "+up3", "+dn3", "-D4"),
    (1536, "-e22", "+fa", "+up2", "+far0", "+dn2", "-fa", "-up1", "-dn1", "+fb", "+far1"),
    (1792, "-C2", "+D6", "-fb", "-A1", "+B21", "-up3", "-dn3", "+far3", "-B20", "+D3", "+C3"),
    (1024, "-D6", "-D3", "-up2", "+far2", "-dn2", "+fc"),
    (2048, "-C1", "+D5", "-fc", "-A3", "-far0", "-far1", "-B31"),
    (1280, "-D5", "-far3", "-far2", "+fd"),
    (2304, "-C3", "+D7", "-A2", "-fd", "-B21"),
    (768, "-D7"),
)


def key_weights():
    shape = (16, BLK)
    flat = lax.broadcasted_iota(jnp.int32, shape, 0) * BLK + lax.broadcasted_iota(jnp.int32, shape, 1)
    own = jnp.where(flat < T, 1.0, 0.0)
    weight = jnp.ones(shape, jnp.float32)
    for level in range(1, 5):
        weight += jnp.where(lax.rem(flat, 1 << level) == 0, own, 0.0)
    for name, top in (("A0", 4), ("B30", 3), ("B20", 3), ("C0", 2), ("C1", 2), ("C2", 2), ("C3", 2), ("A1", 2)):
        base = ROW[name]
        low = top if name == "A1" else top - 1
        weight += jnp.where((flat >= base) & (flat < base + 32), top - 1.0, 0.0)
        weight += jnp.where((flat >= base + 32) & (flat < base + 64), low - 1.0, 0.0)
    return weight


class Links:
    def __init__(self, send_sem, recv_sem):
        self.send_sem, self.recv_sem, self.count, self.sent = send_sem, recv_sem, 0, []

    def make(self, src, dst, device):
        i = self.count
        assert i < N_COPIES
        self.count += 1
        return pltpu.make_async_remote_copy(
            src_ref=src,
            dst_ref=dst,
            send_sem=self.send_sem.at[i],
            recv_sem=self.recv_sem.at[i],
            device_id=device,
            device_id_type=MESH,
        )


def kernel(
    q_hbm, k_hbm, v_hbm, o_ref,
    ch, snd, qv, qm, acc, ms, blk, rb, weights, send_sem, recv_sem, loc_sem,
):
    inner, outer = lax.axis_index("inner"), lax.axis_index("outer")
    y, xh = lax.rem(inner, 4), lax.div(inner, 4)
    core = lax.rem(outer, 2)
    z = lax.rem(lax.div(outer, 2), 4)
    xl = lax.div(outer, 8)
    x = xh * 2 + xl

    def dev(x, y, z, core):
        return (lax.div(x, 2) * 4 + y, lax.rem(x, 2) * 8 + z * 2 + core)

    xs = [lax.rem(x + i, 4) for i in range(4)]
    ys = [y, lax.rem(y, 2) * -2 + 1 + y, lax.rem(y + 2, 4), 3 - y]
    zs = [lax.rem(z + i, 4) for i in range(4)]
    to_core = dev(x, y, z, 1 - core)
    to_x = [None] + [dev(xs[i], y, z, core) for i in (1, 2, 3)]
    to_y = [None] + [dev(x, ys[i], z, core) for i in (1, 2, 3)]
    to_up, to_down = dev(x, y, zs[1], core), dev(x, y, zs[3], core)
    partners = [to_core] + to_x[1:] + to_y[1:] + [to_up, to_down]

    loads = [
        pltpu.make_async_copy(k_hbm, ch.at[0, pl.ds(0, T)], loc_sem.at[0]),
        pltpu.make_async_copy(v_hbm, ch.at[1, pl.ds(0, T)], loc_sem.at[1]),
        pltpu.make_async_copy(q_hbm, qv, loc_sem.at[2]),
    ]
    for load in loads:
        load.start()
    barrier = pltpu.get_barrier_semaphore()
    for device in partners:
        pl.semaphore_signal(barrier, inc=1, device_id=device, device_id_type=MESH)

    grow = lax.broadcasted_iota(jnp.int32, (16, T), 0)
    gcol = lax.broadcasted_iota(jnp.int32, (16, T), 1)
    gpick = jnp.where(gcol == (grow - core * 8) * 64, 1.0, 0.0)
    gpick = jnp.where((grow < 8) == (core == 0), gpick, 0.0).astype(jnp.bfloat16)
    row = lax.broadcasted_iota(jnp.int32, (BLK, T), 0)
    col = lax.broadcasted_iota(jnp.int32, (BLK, T), 1)
    token = jnp.where(
        row < 32,
        row * 16,
        jnp.where(row < 64, row * 16 - 504, jnp.where(row < 128, row * 8 - 508, row * 4 - 510)),
    )
    pick = jnp.where(col == token, 1.0, 0.0).astype(jnp.bfloat16)

    links = Links(send_sem, recv_sem)

    def piece(src_row, dst_row, rows, device, from_snd=False):
        src = snd.at[:, pl.ds(src_row, rows)] if from_snd else ch.at[:, pl.ds(ROW[src_row], rows)]
        return links.make(src, ch.at[:, pl.ds(ROW[dst_row], rows)], device)

    def gpiece(src_row, dst_row, rows, device):
        return links.make(ch.at[core, pl.ds(src_row, rows)], ch.at[core, pl.ds(dst_row, rows)], device)

    copies = {
        "A0": piece(0, "A0", 64, to_y[1], True),
        "B30": piece(0, "B30", 64, to_y[3], True),
        "C0": piece(0, "C0", 64, to_x[2], True),
        "D0": piece(0, "D0", 32, to_core, True),
        "A1": piece(64, "A1", 64, to_y[1], True),
        "B31": piece(64, "B31", 64, to_y[3], True),
        "A2": piece(128, "A2", 64, to_y[1], True),
        "A3": piece(192, "A3", 64, to_y[1], True),
        "B20": piece("A0", "B20", 64, to_y[3]),
        "B21": piece("A1", "B21", 64, to_y[3]),
        "C1": piece("A0", "C1", 64, to_x[2]),
        "C2": piece("B30", "C2", 64, to_x[2]),
        "C3": piece("B20", "C3", 64, to_x[2]),
    }
    for i, name in enumerate(("A0", "B30", "B20", "C0", "C1", "C2", "C3")):
        copies["D%d" % (i + 1)] = piece(name, "D%d" % (i + 1), 32, to_core)
    slot = pl.multiple_of(x * 16, 16)
    copies["e0"] = links.make(blk.at[1 - core], rb, to_core)
    for i in (1, 2, 3):
        copies["e1%d" % i] = gpiece(GA + slot, GA + slot, 16, to_x[i])
        copies["e2%d" % i] = gpiece(GA, GA + i * 64, 64, to_y[i])
    for i in range(4):
        above, below = GBC + i * 128 + 64, GBC + i * 128
        copies["up%d" % i] = gpiece(GA + i * 64, above, 64, to_up)
        copies["dn%d" % i] = gpiece(GA + i * 64, below, 64, to_down)
        copies["far%d" % i] = gpiece(
            below if i % 2 else above, GD + i * 64, 64, to_down if i % 2 else to_up
        )
    for name, at in (("fa", GA), ("fb", GBC), ("fc", GBC + BLK), ("fd", GD)):
        copies[name] = gpiece(at, at, BLK, to_core)

    def act(tokens):
        for token in tokens:
            copy = copies[token[1:]]
            if token[0] == "+":
                copy.start()
            else:
                copy.wait_recv()
                if token == "-e0":
                    ch[core, pl.ds(pl.multiple_of(GA + slot, 16), 16), :] = blk[core] + rb[...]

    for i in range(2):
        loads[i].wait()
        blk[i] = jnp.dot(gpick, ch[i, 0:T, :], preferred_element_type=jnp.float32).astype(jnp.bfloat16)
    pl.semaphore_wait(barrier, len(partners))
    act(FIRST)
    for i in range(2):
        own = ch[i, 0:T, :]
        snd[i] = jnp.dot(pick, own, preferred_element_type=jnp.float32).astype(jnp.bfloat16)
    act(SECOND)

    lane = lax.broadcasted_iota(jnp.int32, (1, 128), 1)
    loads[2].wait()
    for p in range(HEADS // 2):
        q = qv[:, p * 128 : (p + 1) * 128] * jnp.bfloat16(HEAD_DIM**-0.5)
        zero = jnp.zeros_like(q)
        qm[2 * p] = jnp.where(lane < 64, q, zero)
        qm[2 * p + 1] = jnp.where(lane < 64, zero, q)
    weights[...] = key_weights()
    acc[...] = jnp.zeros_like(acc)
    ms[...] = jnp.full_like(ms, -1e30)

    def attend(r0):
        rows = pl.ds(pl.multiple_of(r0, BLK), BLK)
        weight = weights[pl.ds(lax.div(r0, BLK), 1), :]
        for p in range(HEADS // 2):
            keys = ch[0, rows, p * 128 : (p + 1) * 128]
            vals = ch[1, rows, p * 128 : (p + 1) * 128]
            one = jnp.ones_like(vals)
            for h in range(2):
                n = 2 * p + h
                vx = jnp.where(lane < 64, vals, one) if h == 0 else jnp.where(lane < 64, one, vals)
                s = lax.dot_general(
                    qm[n], keys, (((1,), (1,)), ((), ())), preferred_element_type=jnp.float32
                )
                old = ms[n]
                new = jnp.maximum(old, jnp.max(s, axis=1, keepdims=True))
                e = jnp.exp(s - jnp.concatenate([new, new], axis=1)) * weight
                acc[n] = acc[n] * jnp.exp(old - new) + jnp.dot(
                    e.astype(jnp.bfloat16), vx, preferred_element_type=jnp.float32
                )
                ms[n] = new

    def step(j, carry):
        for i, (_, *tokens) in enumerate(STEPS):
            if tokens:
                pl.when(j == i)(lambda tokens=tokens: act(tokens))
        attend(sum(jnp.where(j == i, at, 0) for i, (at, *_) in enumerate(STEPS)))
        return carry

    lax.fori_loop(0, len(STEPS), step, 0)

    for p in range(HEADS // 2):
        lo, hi = acc[2 * p], acc[2 * p + 1]
        both = jnp.where(lane < 64, lo, hi) / pltpu.roll(jnp.where(lane < 64, hi, lo), 64, 1)
        o_ref[:, p * 128 : (p + 1) * 128] = both.astype(jnp.bfloat16)
    for copy in copies.values():
        copy.wait_send()


N_COPIES = 43


def local(queries, key_rows, values, out_weight):
    hbm = pl.BlockSpec(memory_space=pltpu.HBM)
    vmem = pl.BlockSpec(memory_space=pltpu.VMEM)
    bf16, f32 = jnp.bfloat16, jnp.float32
    attended = pl.pallas_call(
        kernel,
        out_shape=jax.ShapeDtypeStruct((T, D), bf16),
        in_specs=[hbm] * 3,
        out_specs=vmem,
        scratch_shapes=[
            pltpu.VMEM((2, 2560, D), bf16),
            pltpu.VMEM((2, BLK, D), bf16),
            pltpu.VMEM((T, D), bf16),
            pltpu.VMEM((HEADS, T, 128), bf16),
            pltpu.VMEM((HEADS, T, 128), f32),
            pltpu.VMEM((HEADS, T, 128), f32),
            pltpu.VMEM((2, 16, D), bf16),
            pltpu.VMEM((16, D), bf16),
            pltpu.VMEM((16, BLK), f32),
            pltpu.SemaphoreType.DMA((N_COPIES,)),
            pltpu.SemaphoreType.DMA((N_COPIES,)),
            pltpu.SemaphoreType.DMA((3,)),
        ],
        compiler_params=pltpu.CompilerParams(
            collective_id=0, has_side_effects=True, vmem_limit_bytes=60 << 20
        ),
    )(queries[0], key_rows[0], values[0])
    return jnp.dot(attended, out_weight, preferred_element_type=f32).astype(bf16)[None]


def solution(mesh):
    placed = P("outer", "inner", None)
    return jax.shard_map(
        local, mesh=mesh, in_specs=(placed, placed, placed, P()), out_specs=placed, check_vma=False
    )
```

```python
import jax
import jax.numpy as jnp
from jax import lax
from jax.experimental import pallas as pl
from jax.experimental.pallas import tpu as pltpu
from jax.sharding import PartitionSpec as P

HEADS = 12
HEAD_DIM = 64
D = 768
T = 512
MESH = pl.DeviceIdType.MESH
BLK = 256

ROW = {
    "A1": 512,
    "B30": 576,
    "C2": 640,
    "D4": 704,
    "D2": 736,
    "A2": 768,
    "C1": 832,
    "B21": 896,
    "D1": 960,
    "D5": 992,
    "C3": 1024,
    "B31": 1088,
    "A3": 1152,
    "D7": 1216,
    "D3": 1248,
    "A0": 1280,
    "C0": 1344,
    "B20": 1408,
    "D0": 1472,
    "D6": 1504,
    "dn0": 1536,
    "up0": 1600,
    "g0": 1664,
    "e21": 1728,
    "e23": 1792,
    "dn1": 1856,
    "far0": 1920,
    "e22": 1984,
    "up3": 2048,
    "up1": 2112,
    "dn3": 2176,
    "up2": 2240,
    "far2": 2304,
    "far3": 2368,
    "dn2": 2432,
    "far1": 2496,
}
GLOBAL = 1536
FIRST = ("+D0", "+e0", "+A0", "+B30",)
STEPS = (
    (0, "-e0", "+e12", "+e11", "+e13", "+C0", "-D0",),
    (256, ),
    (1536, "-e13", "-e11", "-e12", "+e21", "+A1", "+e23", "+e22", "+dn0", "+up0", "+A2", "+A3", "-A0", "+D1", "+B20", "-B30", "+D2", "+C2", "+C1", "-D1", "-D2", "-C0", "+D4", "-e21", "+dn1", "+up1", "-dn0", "-up0", "+f0", "+far0", "-D4", "-e23", "+dn3", "+up3", "-f0",),
    (512, "-A1", "+B21", "+B31", "-C2", "+D6",),
    (1280, "-dn1", "+far1", "-up1", "-D6", "-B20", "+D3", "+C3", "-dn3", "-far0", "-e22", "+f1", "+dn2", "+far3", "+up2",),
    (1792, "-D3", "-C1", "+D5", "-f1", "-up3",),
    (768, "-A2", "-D5", "-B21", "-far1", "-up2", "+f2", "+far2",),
    (2048, "-f2", "-dn2", "-C3", "+D7", "-A3",),
    (1024, "-D7", "-B31", "-far3", "-far2", "+f3",),
    (2304, "-f3",),
)


def key_weights(weights):
    token = lax.broadcasted_iota(jnp.int32, (T, 128), 0)
    own = jnp.ones((T, 128), jnp.float32)
    for level in range(1, 5):
        own += jnp.where(lax.rem(token, 1 << level) == 0, 1.0, 0.0)
    weights[0:T] = own.astype(jnp.bfloat16)
    weights[T:] = jnp.ones((weights.shape[0] - T, 128), jnp.bfloat16)
    half = jnp.ones((32, 128), jnp.bfloat16)
    for name, top in (("A0", 4), ("B30", 3), ("B20", 3), ("C0", 2), ("C1", 2), ("C2", 2), ("C3", 2), ("A1", 2)):
        base = ROW[name]
        low = top if name == "A1" else top - 1
        weights[base : base + 32] = half * top
        weights[base + 32 : base + 64] = half * low


class Links:
    def __init__(self, send_sem, recv_sem):
        self.send_sem, self.recv_sem, self.count, self.sent = send_sem, recv_sem, 0, []

    def make(self, src, dst, device):
        i = self.count
        assert i < N_COPIES
        self.count += 1
        return pltpu.make_async_remote_copy(
            src_ref=src,
            dst_ref=dst,
            send_sem=self.send_sem.at[i],
            recv_sem=self.recv_sem.at[i],
            device_id=device,
            device_id_type=MESH,
        )


def kernel(
    q_hbm, k_hbm, v_hbm, o_ref,
    ch, snd, qv, qm, acc, ms, blk, rb, weights, send_sem, recv_sem, loc_sem,
):
    inner, outer = lax.axis_index("inner"), lax.axis_index("outer")
    y, xh = lax.rem(inner, 4), lax.div(inner, 4)
    core = lax.rem(outer, 2)
    z = lax.rem(lax.div(outer, 2), 4)
    xl = lax.div(outer, 8)
    x = xh * 2 + xl

    def dev(x, y, z, core):
        return (lax.div(x, 2) * 4 + y, lax.rem(x, 2) * 8 + z * 2 + core)

    xs = [lax.rem(x + i, 4) for i in range(4)]
    ys = [y, lax.rem(y, 2) * -2 + 1 + y, lax.rem(y + 2, 4), 3 - y]
    zs = [lax.rem(z + i, 4) for i in range(4)]
    to_core = dev(x, y, z, 1 - core)
    to_x = [None] + [dev(xs[i], y, z, core) for i in (1, 2, 3)]
    to_y = [None] + [dev(x, ys[i], z, core) for i in (1, 2, 3)]
    to_up, to_down = dev(x, y, zs[1], core), dev(x, y, zs[3], core)
    partners = [to_core] + to_x[1:] + to_y[1:] + [to_up, to_down]

    loads = [
        pltpu.make_async_copy(k_hbm, ch.at[0, pl.ds(0, T)], loc_sem.at[0]),
        pltpu.make_async_copy(v_hbm, ch.at[1, pl.ds(0, T)], loc_sem.at[1]),
        pltpu.make_async_copy(q_hbm, qv, loc_sem.at[2]),
    ]
    for load in loads:
        load.start()
    barrier = pltpu.get_barrier_semaphore()
    for device in partners:
        pl.semaphore_signal(barrier, inc=1, device_id=device, device_id_type=MESH)

    grow = lax.broadcasted_iota(jnp.int32, (16, T), 0)
    gcol = lax.broadcasted_iota(jnp.int32, (16, T), 1)
    gpick = jnp.where(gcol == (grow - core * 8) * 64, 1.0, 0.0)
    gpick = jnp.where((grow < 8) == (core == 0), gpick, 0.0).astype(jnp.bfloat16)
    row = lax.broadcasted_iota(jnp.int32, (BLK, T), 0)
    col = lax.broadcasted_iota(jnp.int32, (BLK, T), 1)
    token = jnp.where(
        row < 32,
        row * 16,
        jnp.where(row < 64, row * 16 - 504, jnp.where(row < 128, row * 8 - 508, row * 4 - 510)),
    )
    pick = jnp.where(col == token, 1.0, 0.0).astype(jnp.bfloat16)

    links = Links(send_sem, recv_sem)

    def piece(src_row, dst_row, rows, device, from_snd=False):
        src = snd.at[:, pl.ds(src_row, rows)] if from_snd else ch.at[:, pl.ds(ROW[src_row], rows)]
        return links.make(src, ch.at[:, pl.ds(ROW[dst_row], rows)], device)

    def gpiece(src_row, dst_row, rows, device):
        return links.make(ch.at[core, pl.ds(src_row, rows)], ch.at[core, pl.ds(dst_row, rows)], device)

    copies = {
        "A0": piece(0, "A0", 64, to_y[1], True),
        "B30": piece(0, "B30", 64, to_y[3], True),
        "C0": piece(0, "C0", 64, to_x[2], True),
        "D0": piece(0, "D0", 32, to_core, True),
        "A1": piece(64, "A1", 64, to_y[1], True),
        "B31": piece(64, "B31", 64, to_y[3], True),
        "A2": piece(128, "A2", 64, to_y[1], True),
        "A3": piece(192, "A3", 64, to_y[1], True),
        "B20": piece("A0", "B20", 64, to_y[3]),
        "B21": piece("A1", "B21", 64, to_y[3]),
        "C1": piece("A0", "C1", 64, to_x[2]),
        "C2": piece("B30", "C2", 64, to_x[2]),
        "C3": piece("B20", "C3", 64, to_x[2]),
    }
    for i, name in enumerate(("A0", "B30", "B20", "C0", "C1", "C2", "C3")):
        copies["D%d" % (i + 1)] = piece(name, "D%d" % (i + 1), 32, to_core)
    own_slot = pl.multiple_of(ROW["g0"] + x * 16, 16)
    copies["e0"] = links.make(blk.at[1 - core], rb, to_core)
    for i in (1, 2, 3):
        copies["e1%d" % i] = gpiece(own_slot, own_slot, 16, to_x[i])
        copies["e2%d" % i] = gpiece(ROW["g0"], ROW["e2%d" % i], 64, to_y[i])
    for i in range(4):
        src = ROW["e2%d" % i] if i else ROW["g0"]
        above, below = ROW["up%d" % i], ROW["dn%d" % i]
        copies["up%d" % i] = gpiece(src, above, 64, to_up)
        copies["dn%d" % i] = gpiece(src, below, 64, to_down)
        copies["far%d" % i] = gpiece(
            below if i % 2 else above, ROW["far%d" % i], 64, to_down if i % 2 else to_up
        )
    for i in range(4):
        at = GLOBAL + i * BLK
        copies["f%d" % i] = gpiece(at, at, BLK, to_core)

    def act(tokens):
        for token in tokens:
            copy = copies[token[1:]]
            if token[0] == "+":
                copy.start()
            else:
                copy.wait_recv()
                if token == "-e0":
                    ch[core, pl.ds(own_slot, 16), :] = blk[core] + rb[...]

    for i in range(2):
        loads[i].wait()
        blk[i] = jnp.dot(gpick, ch[i, 0:T, :], preferred_element_type=jnp.float32).astype(jnp.bfloat16)
    for i in range(2):
        own = ch[i, 0:T, :]
        snd[i] = jnp.dot(pick, own, preferred_element_type=jnp.float32).astype(jnp.bfloat16)

    pl.semaphore_wait(barrier, len(partners))
    act(FIRST)

    lane = lax.broadcasted_iota(jnp.int32, (1, 128), 1)
    loads[2].wait()
    for p in range(HEADS // 2):
        q = qv[:, p * 128 : (p + 1) * 128] * jnp.bfloat16(HEAD_DIM**-0.5)
        zero = jnp.zeros_like(q)
        qm[2 * p] = jnp.where(lane < 64, q, zero)
        qm[2 * p + 1] = jnp.where(lane < 64, zero, q)
    key_weights(weights)
    acc[...] = jnp.zeros_like(acc)
    ms[...] = jnp.full_like(ms, -1e30)

    def attend(r0):
        rows = pl.ds(pl.multiple_of(r0, BLK), BLK)
        for p in range(HEADS // 2):
            keys = ch[0, rows, p * 128 : (p + 1) * 128]
            vals = ch[1, rows, p * 128 : (p + 1) * 128]
            one = weights[rows, :]
            vals = vals * one
            for h in range(2):
                n = 2 * p + h
                vx = jnp.where(lane < 64, vals, one) if h == 0 else jnp.where(lane < 64, one, vals)
                s = lax.dot_general(
                    qm[n], keys, (((1,), (1,)), ((), ())), preferred_element_type=jnp.float32
                )
                old = ms[n]
                new = jnp.maximum(old, jnp.max(s, axis=1, keepdims=True))
                e = jnp.exp(s - jnp.concatenate([new, new], axis=1))
                acc[n] = acc[n] * jnp.exp(old - new) + jnp.dot(
                    e.astype(jnp.bfloat16), vx, preferred_element_type=jnp.float32
                )
                ms[n] = new

    def step(j, carry):
        for i, (_, *tokens) in enumerate(STEPS):
            if tokens:
                pl.when(j == i)(lambda tokens=tokens: act(tokens))
        attend(sum(jnp.where(j == i, at, 0) for i, (at, *_) in enumerate(STEPS)))
        return carry

    lax.fori_loop(0, len(STEPS), step, 0)

    for p in range(HEADS // 2):
        lo, hi = acc[2 * p], acc[2 * p + 1]
        both = jnp.where(lane < 64, lo, hi) / pltpu.roll(jnp.where(lane < 64, hi, lo), 64, 1)
        o_ref[:, p * 128 : (p + 1) * 128] = both.astype(jnp.bfloat16)
    for copy in copies.values():
        copy.wait_send()


N_COPIES = 43


def local(queries, key_rows, values, out_weight):
    hbm = pl.BlockSpec(memory_space=pltpu.HBM)
    vmem = pl.BlockSpec(memory_space=pltpu.VMEM)
    bf16, f32 = jnp.bfloat16, jnp.float32
    attended = pl.pallas_call(
        kernel,
        out_shape=jax.ShapeDtypeStruct((T, D), bf16),
        in_specs=[hbm] * 3,
        out_specs=vmem,
        scratch_shapes=[
            pltpu.VMEM((2, 2560, D), bf16),
            pltpu.VMEM((2, BLK, D), bf16),
            pltpu.VMEM((T, D), bf16),
            pltpu.VMEM((HEADS, T, 128), bf16),
            pltpu.VMEM((HEADS, T, 128), f32),
            pltpu.VMEM((HEADS, T, 128), f32),
            pltpu.VMEM((2, 16, D), bf16),
            pltpu.VMEM((16, D), bf16),
            pltpu.VMEM((2560, 128), bf16),
            pltpu.SemaphoreType.DMA((N_COPIES,)),
            pltpu.SemaphoreType.DMA((N_COPIES,)),
            pltpu.SemaphoreType.DMA((3,)),
        ],
        compiler_params=pltpu.CompilerParams(
            collective_id=0, has_side_effects=True, vmem_limit_bytes=60 << 20
        ),
    )(queries[0], key_rows[0], values[0])
    return jnp.dot(attended, out_weight, preferred_element_type=f32).astype(bf16)[None]


def solution(mesh):
    placed = P("outer", "inner", None)
    return jax.shard_map(
        local, mesh=mesh, in_specs=(placed, placed, placed, P()), out_specs=placed, check_vma=False
    )
```

```python
import jax
import jax.numpy as jnp
from jax import lax
from jax.experimental import pallas as pl
from jax.experimental.pallas import tpu as pltpu
from jax.sharding import PartitionSpec as P

HEADS = 12
HEAD_DIM = 64
D = 768
T = 512
MESH = pl.DeviceIdType.MESH
BLK = 256

ROW = {
    "A1": 512,
    "B30": 576,
    "C2": 640,
    "D4": 704,
    "D2": 736,
    "A2": 768,
    "C1": 832,
    "B21": 896,
    "D1": 960,
    "D5": 992,
    "C3": 1024,
    "B31": 1088,
    "A3": 1152,
    "D7": 1216,
    "D3": 1248,
    "A0": 1280,
    "C0": 1344,
    "B20": 1408,
    "D0": 1472,
    "D6": 1504,
    "dn0": 1536,
    "up0": 1600,
    "g0": 1664,
    "e21": 1728,
    "e23": 1792,
    "dn1": 1856,
    "far0": 1920,
    "e22": 1984,
    "up3": 2048,
    "up1": 2112,
    "dn3": 2176,
    "up2": 2240,
    "far2": 2304,
    "far3": 2368,
    "dn2": 2432,
    "far1": 2496,
}
GLOBAL = 1536
FIRST = ("+D0", "+e0", "+A0", "+B30",)
STEPS = (
    (256, "-e0", "+e12", "+e11", "+e13", "+C0", "-D0",),
    (0, "-e13", "-e11", "-e12", "+e21", "+A1", "+e23", "+e22", "+dn0", "+up0", "+A2",),
    (1536, "+A3", "-A0", "+D1", "+B20", "-B30", "+D2", "+C2", "+C1", "-D1", "-D2", "-C0", "+D4", "-e21", "+dn1", "+up1", "-dn0", "-up0", "+f0", "+far0", "-D4", "-e23", "+dn3", "+up3", "-f0",),
    (512, "-A1", "+B21", "+B31", "-C2", "+D6",),
    (1280, "-dn1", "+far1", "-up1", "-D6", "-B20", "+D3", "+C3", "-dn3", "-far0", "-e22", "+f1", "+dn2", "+far3", "+up2",),
    (1792, "-D3", "-C1", "+D5", "-f1", "-up3",),
    (768, "-A2", "-D5", "-B21", "-far1", "-up2", "+f2", "+far2",),
    (2048, "-f2", "-dn2", "-C3", "+D7",),
    (1024, "-A3", "-D7", "-B31", "-far3", "-far2", "+f3",),
    (2304, "-f3",),
)


def key_weights(weights):
    token = lax.broadcasted_iota(jnp.int32, (T, 128), 0)
    own = jnp.ones((T, 128), jnp.float32)
    for level in range(1, 5):
        own += jnp.where(lax.rem(token, 1 << level) == 0, 1.0, 0.0)
    weights[0:T] = own.astype(jnp.bfloat16)
    weights[T:] = jnp.ones((weights.shape[0] - T, 128), jnp.bfloat16)
    half = jnp.ones((32, 128), jnp.bfloat16)
    for name, top in (("A0", 4), ("B30", 3), ("B20", 3), ("C0", 2), ("C1", 2), ("C2", 2), ("C3", 2), ("A1", 2)):
        base = ROW[name]
        low = top if name == "A1" else top - 1
        weights[base : base + 32] = half * top
        weights[base + 32 : base + 64] = half * low


class Links:
    def __init__(self, send_sem, recv_sem):
        self.send_sem, self.recv_sem, self.count, self.sent = send_sem, recv_sem, 0, []

    def make(self, src, dst, device):
        i = self.count
        assert i < N_COPIES
        self.count += 1
        return pltpu.make_async_remote_copy(
            src_ref=src,
            dst_ref=dst,
            send_sem=self.send_sem.at[i],
            recv_sem=self.recv_sem.at[i],
            device_id=device,
            device_id_type=MESH,
        )


def kernel(
    q_hbm, k_hbm, v_hbm, o_ref,
    ch, snd, qv, qm, acc, ms, blk, rb, weights, send_sem, recv_sem, loc_sem,
):
    inner, outer = lax.axis_index("inner"), lax.axis_index("outer")
    y, xh = lax.rem(inner, 4), lax.div(inner, 4)
    core = lax.rem(outer, 2)
    z = lax.rem(lax.div(outer, 2), 4)
    xl = lax.div(outer, 8)
    x = xh * 2 + xl

    def dev(x, y, z, core):
        return (lax.div(x, 2) * 4 + y, lax.rem(x, 2) * 8 + z * 2 + core)

    xs = [lax.rem(x + i, 4) for i in range(4)]
    ys = [y, lax.rem(y, 2) * -2 + 1 + y, lax.rem(y + 2, 4), 3 - y]
    zs = [lax.rem(z + i, 4) for i in range(4)]
    to_core = dev(x, y, z, 1 - core)
    to_x = [None] + [dev(xs[i], y, z, core) for i in (1, 2, 3)]
    to_y = [None] + [dev(x, ys[i], z, core) for i in (1, 2, 3)]
    to_up, to_down = dev(x, y, zs[1], core), dev(x, y, zs[3], core)
    partners = [to_core] + to_x[1:] + to_y[1:] + [to_up, to_down]

    loads = [
        pltpu.make_async_copy(k_hbm, ch.at[0, pl.ds(0, T)], loc_sem.at[0]),
        pltpu.make_async_copy(v_hbm, ch.at[1, pl.ds(0, T)], loc_sem.at[1]),
        pltpu.make_async_copy(q_hbm, qv, loc_sem.at[2]),
    ]
    for load in loads:
        load.start()
    barrier = pltpu.get_barrier_semaphore()
    for device in partners:
        pl.semaphore_signal(barrier, inc=1, device_id=device, device_id_type=MESH)

    grow = lax.broadcasted_iota(jnp.int32, (16, T), 0)
    gcol = lax.broadcasted_iota(jnp.int32, (16, T), 1)
    gpick = jnp.where(gcol == (grow - core * 8) * 64, 1.0, 0.0)
    gpick = jnp.where((grow < 8) == (core == 0), gpick, 0.0).astype(jnp.bfloat16)
    row = lax.broadcasted_iota(jnp.int32, (BLK, T), 0)
    col = lax.broadcasted_iota(jnp.int32, (BLK, T), 1)
    token = jnp.where(
        row < 32,
        row * 16,
        jnp.where(row < 64, row * 16 - 504, jnp.where(row < 128, row * 8 - 508, row * 4 - 510)),
    )
    pick = jnp.where(col == token, 1.0, 0.0).astype(jnp.bfloat16)

    links = Links(send_sem, recv_sem)

    def piece(src_row, dst_row, rows, device, from_snd=False):
        src = snd.at[:, pl.ds(src_row, rows)] if from_snd else ch.at[:, pl.ds(ROW[src_row], rows)]
        return links.make(src, ch.at[:, pl.ds(ROW[dst_row], rows)], device)

    def gpiece(src_row, dst_row, rows, device):
        return links.make(ch.at[core, pl.ds(src_row, rows)], ch.at[core, pl.ds(dst_row, rows)], device)

    copies = {
        "A0": piece(0, "A0", 64, to_y[1], True),
        "B30": piece(0, "B30", 64, to_y[3], True),
        "C0": piece(0, "C0", 64, to_x[2], True),
        "D0": piece(0, "D0", 32, to_core, True),
        "A1": piece(64, "A1", 64, to_y[1], True),
        "B31": piece(64, "B31", 64, to_y[3], True),
        "A2": piece(128, "A2", 64, to_y[1], True),
        "A3": piece(192, "A3", 64, to_y[1], True),
        "B20": piece("A0", "B20", 64, to_y[3]),
        "B21": piece("A1", "B21", 64, to_y[3]),
        "C1": piece("A0", "C1", 64, to_x[2]),
        "C2": piece("B30", "C2", 64, to_x[2]),
        "C3": piece("B20", "C3", 64, to_x[2]),
    }
    for i, name in enumerate(("A0", "B30", "B20", "C0", "C1", "C2", "C3")):
        copies["D%d" % (i + 1)] = piece(name, "D%d" % (i + 1), 32, to_core)
    own_slot = pl.multiple_of(ROW["g0"] + x * 16, 16)
    copies["e0"] = links.make(blk.at[1 - core], rb, to_core)
    for i in (1, 2, 3):
        copies["e1%d" % i] = gpiece(own_slot, own_slot, 16, to_x[i])
        copies["e2%d" % i] = gpiece(ROW["g0"], ROW["e2%d" % i], 64, to_y[i])
    for i in range(4):
        src = ROW["e2%d" % i] if i else ROW["g0"]
        above, below = ROW["up%d" % i], ROW["dn%d" % i]
        copies["up%d" % i] = gpiece(src, above, 64, to_up)
        copies["dn%d" % i] = gpiece(src, below, 64, to_down)
        copies["far%d" % i] = gpiece(
            below if i % 2 else above, ROW["far%d" % i], 64, to_down if i % 2 else to_up
        )
    for i in range(4):
        at = GLOBAL + i * BLK
        copies["f%d" % i] = gpiece(at, at, BLK, to_core)

    def act(tokens):
        for token in tokens:
            copy = copies[token[1:]]
            if token[0] == "+":
                copy.start()
            else:
                copy.wait_recv()
                if token == "-e0":
                    ch[core, pl.ds(own_slot, 16), :] = blk[core] + rb[...]

    for i in range(2):
        loads[i].wait()
        blk[i] = jnp.dot(gpick, ch[i, 0:T, :], preferred_element_type=jnp.float32).astype(jnp.bfloat16)
    for i in range(2):
        own = ch[i, 0:T, :]
        snd[i] = jnp.dot(pick, own, preferred_element_type=jnp.float32).astype(jnp.bfloat16)

    pl.semaphore_wait(barrier, len(partners))
    act(FIRST)

    lane = lax.broadcasted_iota(jnp.int32, (1, 128), 1)
    loads[2].wait()
    for p in range(HEADS // 2):
        q = qv[:, p * 128 : (p + 1) * 128] * jnp.bfloat16(HEAD_DIM**-0.5)
        zero = jnp.zeros_like(q)
        qm[2 * p] = jnp.where(lane < 64, q, zero)
        qm[2 * p + 1] = jnp.where(lane < 64, zero, q)
    key_weights(weights)
    acc[...] = jnp.zeros_like(acc)
    ms[...] = jnp.full_like(ms, -1e30)

    def attend(r0):
        rows = pl.ds(pl.multiple_of(r0, BLK), BLK)
        for p in range(HEADS // 2):
            keys = ch[0, rows, p * 128 : (p + 1) * 128]
            vals = ch[1, rows, p * 128 : (p + 1) * 128]
            one = weights[rows, :]
            vals = vals * one
            for h in range(2):
                n = 2 * p + h
                vx = jnp.where(lane < 64, vals, one) if h == 0 else jnp.where(lane < 64, one, vals)
                s = lax.dot_general(
                    qm[n], keys, (((1,), (1,)), ((), ())), preferred_element_type=jnp.float32
                )
                old = ms[n]
                new = jnp.maximum(old, jnp.max(s, axis=1, keepdims=True))
                e = jnp.exp(s - jnp.concatenate([new, new], axis=1))
                acc[n] = acc[n] * jnp.exp(old - new) + jnp.dot(
                    e.astype(jnp.bfloat16), vx, preferred_element_type=jnp.float32
                )
                ms[n] = new

    def step(j, carry):
        for i, (_, *tokens) in enumerate(STEPS):
            if tokens:
                pl.when(j == i)(lambda tokens=tokens: act(tokens))
        attend(sum(jnp.where(j == i, at, 0) for i, (at, *_) in enumerate(STEPS)))
        return carry

    lax.fori_loop(0, len(STEPS), step, 0)

    for p in range(HEADS // 2):
        lo, hi = acc[2 * p], acc[2 * p + 1]
        both = jnp.where(lane < 64, lo, hi) / pltpu.roll(jnp.where(lane < 64, hi, lo), 64, 1)
        o_ref[:, p * 128 : (p + 1) * 128] = both.astype(jnp.bfloat16)
    for copy in copies.values():
        copy.wait_send()


N_COPIES = 43


def local(queries, key_rows, values, out_weight):
    hbm = pl.BlockSpec(memory_space=pltpu.HBM)
    vmem = pl.BlockSpec(memory_space=pltpu.VMEM)
    bf16, f32 = jnp.bfloat16, jnp.float32
    attended = pl.pallas_call(
        kernel,
        out_shape=jax.ShapeDtypeStruct((T, D), bf16),
        in_specs=[hbm] * 3,
        out_specs=vmem,
        scratch_shapes=[
            pltpu.VMEM((2, 2560, D), bf16),
            pltpu.VMEM((2, BLK, D), bf16),
            pltpu.VMEM((T, D), bf16),
            pltpu.VMEM((HEADS, T, 128), bf16),
            pltpu.VMEM((HEADS, T, 128), f32),
            pltpu.VMEM((HEADS, T, 128), f32),
            pltpu.VMEM((2, 16, D), bf16),
            pltpu.VMEM((16, D), bf16),
            pltpu.VMEM((2560, 128), bf16),
            pltpu.SemaphoreType.DMA((N_COPIES,)),
            pltpu.SemaphoreType.DMA((N_COPIES,)),
            pltpu.SemaphoreType.DMA((3,)),
        ],
        compiler_params=pltpu.CompilerParams(
            collective_id=0, has_side_effects=True, vmem_limit_bytes=53 << 20
        ),
    )(queries[0], key_rows[0], values[0])
    return jnp.dot(attended, out_weight, preferred_element_type=f32).astype(bf16)[None]


def solution(mesh):
    placed = P("outer", "inner", None)
    return jax.shard_map(
        local, mesh=mesh, in_specs=(placed, placed, placed, P()), out_specs=placed, check_vma=False
    )
```

```python
import jax
import jax.numpy as jnp
from jax import lax
from jax.experimental import pallas as pl
from jax.experimental.pallas import tpu as pltpu
from jax.sharding import PartitionSpec as P

HEADS = 12
HEAD_DIM = 64
D = 768
T = 512
MESH = pl.DeviceIdType.MESH
BLK = 256

ROW = {
    "A1": 512,
    "B30": 576,
    "C2": 640,
    "D4": 704,
    "D2": 736,
    "A2": 768,
    "C1": 832,
    "B21": 896,
    "D1": 960,
    "D5": 992,
    "C3": 1024,
    "B31": 1088,
    "A3": 1152,
    "D7": 1216,
    "D3": 1248,
    "A0": 1280,
    "C0": 1344,
    "B20": 1408,
    "D0": 1472,
    "D6": 1504,
    "dn0": 1536,
    "up0": 1600,
    "g0": 1664,
    "e21": 1728,
    "e23": 1792,
    "dn1": 1856,
    "far0": 1920,
    "e22": 1984,
    "up3": 2048,
    "up1": 2112,
    "dn3": 2176,
    "up2": 2240,
    "far2": 2304,
    "far3": 2368,
    "dn2": 2432,
    "far1": 2496,
}
GLOBAL = 1536
FIRST = ("+D0", "+e0", "+A0", "+B30",)
STEPS = (
    (256, "-e0", "+e12", "+e11", "+e13", "+C0", "-D0",),
    (0, "-e13", "-e11", "-e12", "+e21", "+A1", "+e23", "+e22", "+dn0", "+up0", "+A2",),
    (1536, "+A3", "-A0", "+D1", "+B20", "-B30", "+D2", "+C2", "+C1", "-D1", "-D2", "-C0", "+D4", "-e21", "+dn1", "+up1", "-dn0", "-up0", "+f0", "+far0", "-D4", "-e23", "+dn3", "+up3", "-f0",),
    (512, "-A1", "+B21", "+B31", "-C2", "+D6",),
    (1280, "-dn1", "+far1", "-up1", "-D6", "-B20", "+D3", "+C3", "-dn3", "-far0", "-e22", "+f1", "+dn2", "+far3", "+up2",),
    (1792, "-D3", "-C1", "+D5", "-f1", "-up3",),
    (768, "-A2", "-D5", "-B21", "-far1", "-up2", "+f2", "+far2",),
    (2048, "-f2", "-dn2", "-C3", "+D7",),
    (1024, "-A3", "-D7", "-B31", "-far3", "-far2", "+f3",),
    (2304, "-f3",),
)


def key_weights(weights):
    token = lax.broadcasted_iota(jnp.int32, (T, 128), 0)
    own = jnp.ones((T, 128), jnp.float32)
    for level in range(1, 5):
        own += jnp.where(lax.rem(token, 1 << level) == 0, 1.0, 0.0)
    weights[0:T] = own.astype(jnp.bfloat16)
    weights[T:] = jnp.ones((weights.shape[0] - T, 128), jnp.bfloat16)
    half = jnp.ones((32, 128), jnp.bfloat16)
    for name, top in (("A0", 4), ("B30", 3), ("B20", 3), ("C0", 2), ("C1", 2), ("C2", 2), ("C3", 2), ("A1", 2)):
        base = ROW[name]
        low = top if name == "A1" else top - 1
        weights[base : base + 32] = half * top
        weights[base + 32 : base + 64] = half * low


class Links:
    def __init__(self, send_sem, recv_sem):
        self.send_sem, self.recv_sem, self.count, self.sent = send_sem, recv_sem, 0, []

    def make(self, src, dst, device):
        i = self.count
        assert i < N_COPIES
        self.count += 1
        return pltpu.make_async_remote_copy(
            src_ref=src,
            dst_ref=dst,
            send_sem=self.send_sem.at[i],
            recv_sem=self.recv_sem.at[i],
            device_id=device,
            device_id_type=MESH,
        )


def kernel(
    q_hbm, k_hbm, v_hbm, o_ref,
    ch, snd, qv, qm, acc, ms, blk, rb, weights, send_sem, recv_sem, loc_sem,
):
    inner, outer = lax.axis_index("inner"), lax.axis_index("outer")
    y, xh = lax.rem(inner, 4), lax.div(inner, 4)
    core = lax.rem(outer, 2)
    z = lax.rem(lax.div(outer, 2), 4)
    xl = lax.div(outer, 8)
    x = xh * 2 + xl

    def dev(x, y, z, core):
        return (lax.div(x, 2) * 4 + y, lax.rem(x, 2) * 8 + z * 2 + core)

    xs = [lax.rem(x + i, 4) for i in range(4)]
    ys = [y, lax.rem(y, 2) * -2 + 1 + y, lax.rem(y + 2, 4), 3 - y]
    zs = [lax.rem(z + i, 4) for i in range(4)]
    to_core = dev(x, y, z, 1 - core)
    to_x = [None] + [dev(xs[i], y, z, core) for i in (1, 2, 3)]
    to_y = [None] + [dev(x, ys[i], z, core) for i in (1, 2, 3)]
    to_up, to_down = dev(x, y, zs[1], core), dev(x, y, zs[3], core)
    partners = [to_core] + to_x[1:] + to_y[1:] + [to_up, to_down]

    loads = [
        pltpu.make_async_copy(k_hbm, ch.at[0, pl.ds(0, T)], loc_sem.at[0]),
        pltpu.make_async_copy(v_hbm, ch.at[1, pl.ds(0, T)], loc_sem.at[1]),
        pltpu.make_async_copy(q_hbm, qv, loc_sem.at[2]),
    ]
    for load in loads:
        load.start()
    barrier = pltpu.get_barrier_semaphore()
    for device in partners:
        pl.semaphore_signal(barrier, inc=1, device_id=device, device_id_type=MESH)

    grow = lax.broadcasted_iota(jnp.int32, (16, T), 0)
    gcol = lax.broadcasted_iota(jnp.int32, (16, T), 1)
    gpick = jnp.where(gcol == (grow - core * 8) * 64, 1.0, 0.0)
    gpick = jnp.where((grow < 8) == (core == 0), gpick, 0.0).astype(jnp.bfloat16)
    row = lax.broadcasted_iota(jnp.int32, (BLK, T), 0)
    col = lax.broadcasted_iota(jnp.int32, (BLK, T), 1)
    token = jnp.where(
        row < 32,
        row * 16,
        jnp.where(row < 64, row * 16 - 504, jnp.where(row < 128, row * 8 - 508, row * 4 - 510)),
    )
    pick = jnp.where(col == token, 1.0, 0.0).astype(jnp.bfloat16)

    links = Links(send_sem, recv_sem)

    def piece(src_row, dst_row, rows, device, from_snd=False):
        src = snd.at[:, pl.ds(src_row, rows)] if from_snd else ch.at[:, pl.ds(ROW[src_row], rows)]
        return links.make(src, ch.at[:, pl.ds(ROW[dst_row], rows)], device)

    def gpiece(src_row, dst_row, rows, device):
        return links.make(ch.at[core, pl.ds(src_row, rows)], ch.at[core, pl.ds(dst_row, rows)], device)

    copies = {
        "A0": piece(0, "A0", 64, to_y[1], True),
        "B30": piece(0, "B30", 64, to_y[3], True),
        "C0": piece(0, "C0", 64, to_x[2], True),
        "D0": piece(0, "D0", 32, to_core, True),
        "A1": piece(64, "A1", 64, to_y[1], True),
        "B31": piece(64, "B31", 64, to_y[3], True),
        "A2": piece(128, "A2", 64, to_y[1], True),
        "A3": piece(192, "A3", 64, to_y[1], True),
        "B20": piece("A0", "B20", 64, to_y[3]),
        "B21": piece("A1", "B21", 64, to_y[3]),
        "C1": piece("A0", "C1", 64, to_x[2]),
        "C2": piece("B30", "C2", 64, to_x[2]),
        "C3": piece("B20", "C3", 64, to_x[2]),
    }
    for i, name in enumerate(("A0", "B30", "B20", "C0", "C1", "C2", "C3")):
        copies["D%d" % (i + 1)] = piece(name, "D%d" % (i + 1), 32, to_core)
    own_slot = pl.multiple_of(ROW["g0"] + x * 16, 16)
    copies["e0"] = links.make(blk.at[1 - core], rb, to_core)
    for i in (1, 2, 3):
        copies["e1%d" % i] = gpiece(own_slot, own_slot, 16, to_x[i])
        copies["e2%d" % i] = gpiece(ROW["g0"], ROW["e2%d" % i], 64, to_y[i])
    for i in range(4):
        src = ROW["e2%d" % i] if i else ROW["g0"]
        above, below = ROW["up%d" % i], ROW["dn%d" % i]
        copies["up%d" % i] = gpiece(src, above, 64, to_up)
        copies["dn%d" % i] = gpiece(src, below, 64, to_down)
        copies["far%d" % i] = gpiece(
            below if i % 2 else above, ROW["far%d" % i], 64, to_down if i % 2 else to_up
        )
    for i in range(4):
        at = GLOBAL + i * BLK
        copies["f%d" % i] = gpiece(at, at, BLK, to_core)

    def act(tokens):
        for token in tokens:
            copy = copies[token[1:]]
            if token[0] == "+":
                copy.start()
            else:
                copy.wait_recv()
                if token == "-e0":
                    ch[core, pl.ds(own_slot, 16), :] = blk[core] + rb[...]

    for i in range(2):
        loads[i].wait()
        blk[i] = jnp.dot(gpick, ch[i, 0:T, :], preferred_element_type=jnp.float32).astype(jnp.bfloat16)
    for i in range(2):
        own = ch[i, 0:T, :]
        snd[i] = jnp.dot(pick, own, preferred_element_type=jnp.float32).astype(jnp.bfloat16)

    key_weights(weights)
    acc[...] = jnp.zeros_like(acc)
    ms[...] = jnp.full_like(ms, -1e30)
    pl.semaphore_wait(barrier, len(partners))
    act(FIRST)

    lane = lax.broadcasted_iota(jnp.int32, (1, 128), 1)
    loads[2].wait()
    for p in range(HEADS // 2):
        q = qv[:, p * 128 : (p + 1) * 128] * jnp.bfloat16(HEAD_DIM**-0.5)
        zero = jnp.zeros_like(q)
        qm[2 * p] = jnp.where(lane < 64, q, zero)
        qm[2 * p + 1] = jnp.where(lane < 64, zero, q)

    def attend(r0):
        rows = pl.ds(pl.multiple_of(r0, BLK), BLK)
        for p in range(HEADS // 2):
            keys = ch[0, rows, p * 128 : (p + 1) * 128]
            vals = ch[1, rows, p * 128 : (p + 1) * 128]
            one = weights[rows, :]
            vals = vals * one
            for h in range(2):
                n = 2 * p + h
                vx = jnp.where(lane < 64, vals, one) if h == 0 else jnp.where(lane < 64, one, vals)
                s = lax.dot_general(
                    qm[n], keys, (((1,), (1,)), ((), ())), preferred_element_type=jnp.float32
                )
                old = ms[n]
                new = jnp.maximum(old, jnp.max(s, axis=1, keepdims=True))
                e = jnp.exp(s - jnp.concatenate([new, new], axis=1))
                acc[n] = acc[n] * jnp.exp(old - new) + jnp.dot(
                    e.astype(jnp.bfloat16), vx, preferred_element_type=jnp.float32
                )
                ms[n] = new

    def step(j, carry):
        for i, (_, *tokens) in enumerate(STEPS):
            if tokens:
                pl.when(j == i)(lambda tokens=tokens: act(tokens))
        attend(sum(jnp.where(j == i, at, 0) for i, (at, *_) in enumerate(STEPS)))
        return carry

    lax.fori_loop(0, len(STEPS), step, 0)

    for p in range(HEADS // 2):
        lo, hi = acc[2 * p], acc[2 * p + 1]
        both = jnp.where(lane < 64, lo, hi) / pltpu.roll(jnp.where(lane < 64, hi, lo), 64, 1)
        o_ref[:, p * 128 : (p + 1) * 128] = both.astype(jnp.bfloat16)
    for copy in copies.values():
        copy.wait_send()


N_COPIES = 43


def local(queries, key_rows, values, out_weight):
    hbm = pl.BlockSpec(memory_space=pltpu.HBM)
    vmem = pl.BlockSpec(memory_space=pltpu.VMEM)
    bf16, f32 = jnp.bfloat16, jnp.float32
    attended = pl.pallas_call(
        kernel,
        out_shape=jax.ShapeDtypeStruct((T, D), bf16),
        in_specs=[hbm] * 3,
        out_specs=vmem,
        scratch_shapes=[
            pltpu.VMEM((2, 2560, D), bf16),
            pltpu.VMEM((2, BLK, D), bf16),
            pltpu.VMEM((T, D), bf16),
            pltpu.VMEM((HEADS, T, 128), bf16),
            pltpu.VMEM((HEADS, T, 128), f32),
            pltpu.VMEM((HEADS, T, 128), f32),
            pltpu.VMEM((2, 16, D), bf16),
            pltpu.VMEM((16, D), bf16),
            pltpu.VMEM((2560, 128), bf16),
            pltpu.SemaphoreType.DMA((N_COPIES,)),
            pltpu.SemaphoreType.DMA((N_COPIES,)),
            pltpu.SemaphoreType.DMA((3,)),
        ],
        compiler_params=pltpu.CompilerParams(
            collective_id=0, has_side_effects=True, vmem_limit_bytes=53 << 20
        ),
    )(queries[0], key_rows[0], values[0])
    return jnp.dot(attended, out_weight, preferred_element_type=f32).astype(bf16)[None]


def solution(mesh):
    placed = P("outer", "inner", None)
    return jax.shard_map(
        local, mesh=mesh, in_specs=(placed, placed, placed, P()), out_specs=placed, check_vma=False
    )
```
